768 devices in a mesh: gx: 8 (over x, core), gy: 96 (over y, z).
Axes of the slice: x: 4, y: 8, z: 12, core: 2. Of those that a mesh axis runs over, the one named last changes fastest.
Arguments:
- chi: float32 [384, 64, 256], P('gy', 'gx'), may hold values from -6 to 6
- sigma: float32 [384, 64, 256], P('gy', 'gx'), may hold values from 25 to 250
- vertical: float32 [4, 64, 64], replicated, may hold values from -0.75 to 0.75
- kx: float32 [384, 64, 256], P('gy', 'gx'), may hold values from 16 to 480
- ky: float32 [384, 64, 256], P('gy', 'gx'), may hold values from 1024 to 30720
Outputs:
- increment: float32 [384, 64, 256], P('gy', 'gx')
The draws below stay inside these ranges and needn't reach their ends.
All inputs are finite; a program needn't handle non-finite values.
Results may differ from the reference program's by a relative error of at most 0.0003.
Values sent between devices are 32-bit elements; how exact they have to be, the bound alone decides.
No kernel may reach another device: no remote copies, remote signals or barrier semaphores. Data moves between devices by JAX's collectives and lax.ppermute only.
A program may use at most 64 MiB of HBM per device.

```python
import math
import jax
import jax.numpy as jnp
from jax import lax

F = 4
L = 64
ITERS = 3
FL = 256
NX = 64
NY = 384


def level_of(stream_key, shape, cuts, low, top_value):
    loudness = 1.0
    for axis_at, parts in cuts:
        heights = jax.random.uniform(jax.random.fold_in(jax.random.fold_in(stream_key, 6), axis_at), (parts,), jnp.float32, low / len(cuts), top_value / len(cuts))
        loudness = loudness * jnp.repeat(jnp.exp(heights), shape[axis_at] // parts).reshape((-1,) + (1,) * (len(shape) - 1 - axis_at))
    return loudness


def scatter_about(rng, dims, scale, limit, pieces=(), held_as=jnp.bfloat16):
    values = scale * jax.random.normal(rng, dims, jnp.float32)
    if pieces:
        values = values * level_of(rng, dims, pieces, -0.22, 0.18)
    return jnp.clip(values, -limit, limit).astype(held_as)


def setup_inputs(seed: int = 0) -> dict:
    key_list = jax.random.split(jax.random.key(seed), 6)
    return {
        "chi": scatter_about(key_list[0], (NY, NX, FL), 1.0, 6.0, ((0, 96), (1, 8)), jnp.float32),
        "sigma": jnp.clip(jnp.exp(math.log(250.0) - 2.3025851 * jax.random.uniform(key_list[1], (NY, NX, FL), jnp.float32) ** level_of(key_list[1], (NY, NX, FL), ((0, 96), (1, 8)), -0.2, 0.2)), 25.0, 250.0),
        "vertical": scatter_about(key_list[2], (F, L, L), L ** -0.5, 0.75, (), jnp.float32),
        "kx": jnp.clip(jnp.exp(math.log(480.0) - 3.4011974 * jax.random.uniform(key_list[3], (NY, NX, FL), jnp.float32) ** level_of(key_list[3], (NY, NX, FL), ((0, 96), (1, 8)), -0.2, 0.2)), 16.0, 480.0),
        "ky": jnp.clip(jnp.exp(math.log(30720.0) - 3.4011974 * jax.random.uniform(key_list[4], (NY, NX, FL), jnp.float32) ** level_of(key_list[4], (NY, NX, FL), ((0, 96), (1, 8)), -0.2, 0.2)), 1024.0, 30720.0),
    }


def line_solve(values, kleft):
    place = lax.broadcasted_iota(jnp.int32, kleft.shape, 0)
    kleft = jnp.where(place == 0, jnp.zeros_like(kleft), kleft)
    knext = jnp.concatenate([kleft[1:], jnp.zeros_like(kleft[:1])], 0)

    def descend(carry, row):
        excess, eliminated = carry
        conduct, source = row
        pivot = excess + conduct
        new_excess = 1.0 + conduct * excess / pivot
        new_value = source + conduct * eliminated / pivot
        return (new_excess, new_value), (new_excess, new_value)

    start = (jnp.ones_like(values[0]), jnp.zeros_like(values[0]))
    finals, (excesses, reduced) = lax.scan(descend, start, (kleft, values))

    def ascend(carry, row):
        excess, eliminated, conduct = row
        solved_value = (eliminated + conduct * carry) / (excess + conduct)
        return solved_value, solved_value

    ending, solved = lax.scan(ascend, jnp.zeros_like(values[0]), (excesses, reduced, knext), reverse=True)
    return solved


def reference(chi, sigma, vertical, kx, ky):
    fields = vertical.shape[0]
    levels = vertical.shape[1]
    scaled = sigma * chi
    shaped = scaled.reshape(scaled.shape[0], scaled.shape[1], fields, levels)
    mixed = jnp.einsum("yxfl,flk->yxfk", shaped, vertical, precision=lax.Precision.HIGHEST).reshape(scaled.shape)
    current = mixed
    for sweep in range(ITERS):
        current = jnp.swapaxes(line_solve(jnp.swapaxes(current, 0, 1), jnp.swapaxes(kx, 0, 1)), 0, 1)
        current = line_solve(current, ky)
    return current
```

```python
import jax
import jax.numpy as jnp
from jax import lax
from jax.experimental import pallas as pl
from jax.experimental.pallas import tpu as pltpu
from jax.sharding import PartitionSpec as P

ROWS = 4
SPAN = 8
PEERS_X = 8
PEERS_Y = 96
LANES = 128
SLOTS = 3
PAIRS = SLOTS * ROWS
HELD = 16
SUMS = 5

f32 = jnp.float32


def spin(value, shift, axis):
    return pltpu.roll(value, shift % value.shape[axis], axis)


def place(value, axis):
    return lax.broadcasted_iota(jnp.int32, value.shape, axis)


def cell(conduct):
    resist = 1.0 / conduct
    one = jnp.ones_like(conduct)
    return (1.0 + resist, one, resist, one)


def joined(later, earlier):
    a2, b2, c2, k2 = later
    a1, b1, c1, k1 = earlier
    scale = 1.0 / (c2 * b1 + 1.0)
    b = (a2 * b1 + b2) * scale
    c = (c2 * a1 + c1) * scale
    k = k1 * k2 * scale
    return (k * k + b * c, b, c, k)


def kept_where(test, port):
    return tuple(jnp.where(test, m, n) for m, n in zip(port, (1.0, 0.0, 0.0, 1.0)))


def prefixes(port, axis, shifts):
    where = place(port[0], axis)
    for s in shifts:
        earlier = kept_where(where >= s, tuple(spin(m, s, axis) for m in port))
        port = joined(port, earlier)
    return port


def suffixes(port, axis, shifts):
    where = place(port[0], axis)
    size = port[0].shape[axis]
    for s in shifts:
        later = kept_where(where < size - s, tuple(spin(m, -s, axis) for m in port))
        port = joined(later, port)
    return port


def totals(port, source, axis, shifts):
    where = place(source, axis)
    current, tension = source, jnp.zeros_like(source)
    for s in shifts:
        test = where >= s
        earlier = kept_where(test, tuple(spin(m, s, axis) for m in port))
        before = jnp.where(test, spin(current, s, axis), 0.0)
        strain = jnp.where(test, spin(tension, s, axis), 0.0)
        a, b, c, k = port
        gain = 1.0 / k
        current, tension = (
            (a * before + b * strain) * gain + current,
            (c * before + strain) * gain + tension,
        )
        port = joined(port, earlier)
    return port[1], port[2], port[3], current, tension


def x_terms(conduct, front, back, excess_in, behind_in):
    where = place(conduct, 1)
    fa, fb, fc = front
    ba, bb, bc = back
    excess = (fa * excess_in + fb) / (fc * excess_in + 1.0)
    behind = (behind_in + bb) / (bc * behind_in + ba)
    excess_before = jnp.where(where == 0, excess_in, spin(excess, 1, 1))
    behind_next = jnp.where(where == SPAN - 1, behind_in, spin(behind, -1, 1))
    up = conduct / (excess_before + conduct)
    down = conduct / (1.0 + behind_next + conduct)
    inverse = 1.0 / (excess + behind_next)
    up1 = jnp.where(where == 0, 0.0, up)
    up2 = up1 * spin(up1, 1, 1)
    up4 = up2 * spin(up2, 2, 1)
    down1 = jnp.where(where == SPAN - 1, 0.0, down)
    down2 = down1 * spin(down1, -1, 1)
    down4 = down2 * spin(down2, -2, 1)
    up_all, down_all = up, down
    for s in (1, 2, 4):
        up_all = up_all * jnp.where(where >= s, spin(up_all, s, 1), 1.0)
        down_all = down_all * jnp.where(where < SPAN - s, spin(down_all, -s, 1), 1.0)
    down_next = jnp.where(where == SPAN - 1, 1.0, spin(down_all, -1, 1))
    return (
        up1,
        up2,
        up4,
        down,
        down1,
        down2,
        down4,
        inverse,
        up_all * inverse,
        down_next * inverse,
    )


X_TERMS = 10


def x_sweep(values, terms):
    up1, up2, up4, down, down1, down2, down4, inverse = terms[:8]
    ahead = values
    back = down * values
    for s, up_s, down_s in ((1, up1, down1), (2, up2, down2), (4, up4, down4)):
        ahead = ahead + up_s * spin(ahead, s, 1)
        back = back + down_s * spin(back, -s, 1)
    back_next = jnp.where(place(back, 1) == SPAN - 1, 0.0, spin(back, -1, 1))
    return (ahead + back_next) * inverse, ahead, back


Y_SHIFTS = (1, 2, 4, 8, 16, 32, 64)
Y_TERMS = 5


def y_terms(conducts):
    lane = place(conducts[0], 1)
    block = cell(conducts[0])
    for conduct in conducts[1:]:
        block = joined(cell(conduct), block)
    block = kept_where(lane < PEERS_Y, block)
    ahead = prefixes(block, 1, Y_SHIFTS)
    back = suffixes(block, 1, Y_SHIFTS)
    excess = jnp.where(lane == 0, 0.0, spin(ahead[1], 1, 1))
    behind = jnp.where(lane == LANES - 1, 0.0, spin(back[1] / back[0], -1, 1))
    ups, downs, excesses, behinds = [], [], [], []
    for conduct in conducts:
        up = conduct / (excess + conduct)
        excess = 1.0 + up * excess
        ups.append(up)
        excesses.append(excess)
    for conduct in reversed(conducts):
        down = conduct / (1.0 + behind + conduct)
        behinds.append(behind)
        downs.append(down)
        behind = down * (1.0 + behind)
    downs, behinds = downs[::-1], behinds[::-1]
    inverses = [1.0 / (e + h) for e, h in zip(excesses, behinds)]
    up_all = [ups[0]]
    for up in ups[1:]:
        up_all.append(up_all[-1] * up)
    down_all = [downs[-1]]
    for down in downs[-2::-1]:
        down_all.append(down_all[-1] * down)
    down_all = down_all[::-1]
    into_up = [m * inverse for m, inverse in zip(up_all, inverses)]
    into_down = [m * inverse for m, inverse in zip(down_all[1:] + [1.0], inverses)]
    up_s = jnp.where(lane == 0, 0.0, up_all[-1])
    down_s = jnp.where(lane >= PEERS_Y - 1, 0.0, down_all[0])
    steps = []
    for s in Y_SHIFTS:
        steps.append((up_s, down_s))
        up_s = up_s * spin(up_s, s, 1)
        down_s = down_s * spin(down_s, -s, 1)
    return (ups, downs, inverses, into_up, into_down), steps


def y_solve(values, terms, steps):
    ups, downs, inverses, into_up, into_down = terms
    lane = place(values[0], 1)
    ahead = [values[0]]
    for value, up in zip(values[1:], ups[1:]):
        ahead.append(value + up * ahead[-1])
    back = [downs[-1] * values[-1]]
    for value, down in zip(values[-2::-1], downs[-2::-1]):
        back.append(down * (value + back[-1]))
    back = back[::-1]
    up_in, down_in = ahead[-1], back[0]
    for s, (up_s, down_s) in zip(Y_SHIFTS, steps):
        up_in = up_in + up_s * spin(up_in, s, 1)
        down_in = down_in + down_s * spin(down_in, -s, 1)
    up_in = jnp.where(lane == 0, 0.0, spin(up_in, 1, 1))
    down_in = jnp.where(lane >= PEERS_Y - 1, 0.0, spin(down_in, -1, 1))
    solved = []
    for j in range(ROWS):
        here = ahead[j] + back[j + 1] if j + 1 < ROWS else ahead[j]
        solved.append(here * inverses[j] + into_up[j] * up_in + into_down[j] * down_in)
    return solved


def packed(field, fill):
    low, high = field[:, :LANES], field[:, LANES:]
    lane = place(low, 1)
    rest = jnp.where(lane < 32, spin(low, 32, 1), spin(high, 64, 1))
    rest = jnp.where(lane < 64, rest, fill)
    return jnp.concatenate([low, high, rest, jnp.zeros_like(low)], 0).T


def unpacked(lines):
    turned = lines.T
    low, high, rest = turned[:32], turned[32:64], turned[64:96]
    lane = place(low, 1)
    low = jnp.where(lane < PEERS_Y, low, spin(rest, 96, 1))
    high = jnp.where(lane < PEERS_Y, high, spin(rest, 64, 1))
    return jnp.concatenate([low, high], 1)


def filled(lines):
    return jnp.concatenate([lines, jnp.zeros((LANES - PEERS_Y, LANES), f32)], 0)


def mix_kernel(chi, sigma, vertical, kx, ky, out):
    scaled = (sigma[...] * chi[...]).reshape(ROWS * SPAN, 256)
    blank = jnp.zeros((64, 64), f32)
    halves = []
    for h in range(2):
        weight = jnp.concatenate(
            [
                jnp.concatenate([vertical[2 * h], blank], 1),
                jnp.concatenate([blank, vertical[2 * h + 1]], 1),
            ],
            0,
        )
        halves.append(
            jnp.dot(
                scaled[:, h * LANES : (h + 1) * LANES],
                weight,
                precision=lax.Precision.HIGHEST,
                preferred_element_type=f32,
            )
        )
    mixed = jnp.concatenate(halves, 1)
    out[:, 0:LANES] = packed(mixed, 0.0)[:PEERS_Y]
    out[:, LANES : 2 * LANES] = packed(kx[...].reshape(ROWS * SPAN, 256), 1.0)[:PEERS_Y]
    out[:, 2 * LANES : 3 * LANES] = packed(ky[...].reshape(ROWS * SPAN, 256), 1.0)[:PEERS_Y]


def sum_kernel(lines, u_out, kx_out, ky_out, out, rows):
    fields = []
    for n in range(3):
        turned = filled(lines[:, n * LANES : (n + 1) * LANES]).T[: PAIRS * SPAN]
        field = turned.reshape(SLOTS, ROWS, SPAN, LANES)
        if n:
            field = jnp.where(place(field, 3) < PEERS_Y, field, 1.0)
        fields.append(field)
    u, kx, ky = fields
    u_out[...] = u
    kx_out[...] = kx
    ky_out[...] = ky
    rows[...] = jnp.ones_like(rows)
    for c in range(SLOTS):
        sums = totals(cell(kx[c]), u[c], 1, (1, 2, 4))
        for n, total in enumerate(sums):
            for j in range(ROWS):
                at = n * HELD + c * ROWS + j
                rows[at : at + 1, :] = total[j, SPAN - 1 : SPAN, :]
    for q in range(PEERS_X):
        out[q] = rows[...]


def term_kernel(kx, ky, front_out, back_out, y_out, step_out):
    for c in range(SLOTS):
        port = cell(kx[c])
        front = prefixes(port, 1, (1, 2, 4))
        back = suffixes(port, 1, (1, 2, 4))
        for n in range(3):
            front_out[n, c] = front[n]
            back_out[n, c] = back[n]
        terms, steps = y_terms([ky[c, j] for j in range(ROWS)])
        for n, members in enumerate(terms):
            for j, member in enumerate(members):
                y_out[n, c, j] = member
        for n, (up_s, down_s) in enumerate(steps):
            step_out[n, c, 0] = up_s
            step_out[n, c, 1] = down_s


def spread(rows, c):
    return jnp.stack(
        [
            jnp.broadcast_to(rows[c * ROWS + j : c * ROWS + j + 1, :], (SPAN, LANES))
            for j in range(ROWS)
        ]
    )


def loaded_y(y_ref, step_ref, c):
    terms = [[y_ref[n, c, j] for j in range(ROWS)] for n in range(Y_TERMS)]
    steps = [(step_ref[n, c, 0], step_ref[n, c, 1]) for n in range(len(Y_SHIFTS))]
    return terms, steps


def send(here, out, up_rows, down_rows):
    ups, downs = up_rows[...], down_rows[...]
    for q in range(PEERS_X):
        out[q] = jnp.where(q > here, ups, downs)


def start_next(c, solved, x_c, pre_out, up_rows, down_rows):
    pre, ahead, back = x_sweep(solved, x_c)
    pre_out[c] = pre
    for j in range(ROWS):
        at = c * ROWS + j
        up_rows[at : at + 1, :] = ahead[j, SPAN - 1 : SPAN, :]
        down_rows[at : at + 1, :] = back[j, 0:1, :]


def first_kernel(
    where, got, u, kx, front, back, y_ref, step_ref,
    out, pre_out, x_out, rate_out, e_in, h_in, f_in, g_in,
):
    here = where[0]

    def member(q, n):
        return got[q, n * HELD : (n + 1) * HELD, :]

    excess = flow = jnp.zeros((HELD, LANES), f32)
    for q in range(PEERS_X):
        b, c, k, current, tension = (member(q, n) for n in range(SUMS))
        scale = 1.0 / (c * excess + 1.0)
        after = ((k * k + b * c) * excess + b) * scale
        rate = k * scale
        passed = current - after * tension + rate * flow
        rate_out[q] = rate
        excess = jnp.where(q < here, after, excess)
        flow = jnp.where(q < here, passed, flow)
    e_in[...] = excess
    f_in[...] = flow
    behind = flow = jnp.zeros((HELD, LANES), f32)
    for q in reversed(range(PEERS_X)):
        b, c, k, current, tension = (member(q, n) for n in range(SUMS))
        scale = 1.0 / (c * behind + (k * k + b * c))
        rate = k * scale
        passed = rate * (flow + current + behind * tension)
        after = (behind + b) * scale
        rate_out[q] = jnp.where(q > here, rate, rate_out[q])
        behind = jnp.where(q > here, after, behind)
        flow = jnp.where(q > here, passed, flow)
    h_in[...] = behind
    g_in[...] = flow
    up_rows, down_rows = f_in, g_in
    entries = [(spread(f_in, c), spread(g_in, c)) for c in range(SLOTS)]
    for c in range(SLOTS):
        terms = x_terms(
            kx[c],
            tuple(front[n, c] for n in range(3)),
            tuple(back[n, c] for n in range(3)),
            spread(e_in, c),
            spread(h_in, c),
        )
        for n in range(X_TERMS):
            x_out[n, c] = terms[n]
        pre, _, _ = x_sweep(u[c], terms)
        solved = pre + terms[8] * entries[c][0] + terms[9] * entries[c][1]
        solved = jnp.stack(y_solve([solved[j] for j in range(ROWS)], *loaded_y(y_ref, step_ref, c)))
        start_next(c, solved, terms, pre_out, up_rows, down_rows)
    send(here, out, up_rows, down_rows)


def entered(here, got, rates, f_in, g_in):
    flow = jnp.zeros((HELD, LANES), f32)
    for q in range(PEERS_X - 1):
        flow = jnp.where(q < here, got[q] + rates[q] * flow, flow)
    f_in[...] = flow
    flow = jnp.zeros((HELD, LANES), f32)
    for q in reversed(range(1, PEERS_X)):
        flow = jnp.where(q > here, got[q] + rates[q] * flow, flow)
    g_in[...] = flow


def solved_slot(c, pre, x_ref, y_ref, step_ref, f_in, g_in):
    solved = pre[c] + x_ref[8, c] * spread(f_in, c) + x_ref[9, c] * spread(g_in, c)
    return y_solve([solved[j] for j in range(ROWS)], *loaded_y(y_ref, step_ref, c))


def middle_kernel(
    where, got, pre, x_ref, rates, y_ref, step_ref,
    out, pre_out, f_in, g_in, up_rows, down_rows,
):
    here = where[0]
    entered(here, got, rates, f_in, g_in)
    up_rows[...] = jnp.zeros_like(up_rows)
    down_rows[...] = jnp.zeros_like(down_rows)
    for c in range(SLOTS):
        solved = jnp.stack(solved_slot(c, pre, x_ref, y_ref, step_ref, f_in, g_in))
        start_next(c, solved, [x_ref[n, c] for n in range(X_TERMS)], pre_out, up_rows, down_rows)
    send(here, out, up_rows, down_rows)


def last_kernel(where, got, pre, x_ref, rates, y_ref, step_ref, out, f_in, g_in):
    entered(where[0], got, rates, f_in, g_in)
    rows = []
    for c in range(SLOTS):
        rows += solved_slot(c, pre, x_ref, y_ref, step_ref, f_in, g_in)
    rows.append(jnp.zeros((LANES - PAIRS * SPAN, LANES), f32))
    out[...] = jnp.concatenate(rows, 0).T[:PEERS_Y]


def return_kernel(lines, out):
    out[...] = unpacked(filled(lines[...])).reshape(ROWS, SPAN, 256)


def call(kernel, shapes, args, scratch=(), name=None, scalars=0):
    vmem = pl.BlockSpec(memory_space=pltpu.VMEM)
    smem = pl.BlockSpec(memory_space=pltpu.SMEM)
    outs = [jax.ShapeDtypeStruct(shape, f32) for shape in shapes]
    got = pl.pallas_call(
        kernel,
        out_shape=outs,
        in_specs=[smem] * scalars + [vmem] * (len(args) - scalars),
        out_specs=[vmem] * len(outs),
        scratch_shapes=[pltpu.VMEM(shape, f32) for shape in scratch],
        compiler_params=pltpu.CompilerParams(vmem_limit_bytes=16 << 20),
        name=name,
    )(*args)
    return got[0] if len(outs) == 1 else got


FIELD = (SLOTS, ROWS, SPAN, LANES)
ENTRY = (HELD, LANES)


def swapped(value, axis):
    return lax.all_to_all(value, axis, split_axis=0, concat_axis=0, tiled=True)


def body(chi, sigma, vertical, kx, ky):
    here = lax.axis_index("gx").astype(jnp.int32).reshape(1)
    lines = call(mix_kernel, [(PEERS_Y, 3 * LANES)], (chi, sigma, vertical, kx, ky), name="mix")
    lines = swapped(lines, "gy")
    u, kx, ky, sums = call(
        sum_kernel,
        [FIELD, FIELD, FIELD, (PEERS_X, SUMS * HELD, LANES)],
        (lines,),
        [(SUMS * HELD, LANES)],
        name="sums",
    )
    front, back, y_ref, steps = call(
        term_kernel,
        [(3, *FIELD), (3, *FIELD), (Y_TERMS, *FIELD), (len(Y_SHIFTS), SLOTS, 2, SPAN, LANES)],
        (kx, ky),
        name="terms",
    )
    got = swapped(sums, "gx")
    sent, pre, x_ref, rates = call(
        first_kernel,
        [(PEERS_X, *ENTRY), FIELD, (X_TERMS, *FIELD), (PEERS_X, *ENTRY)],
        (here, got, u, kx, front, back, y_ref, steps),
        [ENTRY] * 4,
        name="first",
        scalars=1,
    )
    got = swapped(sent, "gx")
    sent, pre = call(
        middle_kernel,
        [(PEERS_X, *ENTRY), FIELD],
        (here, got, pre, x_ref, rates, y_ref, steps),
        [ENTRY] * 4,
        name="middle",
        scalars=1,
    )
    got = swapped(sent, "gx")
    lines = call(
        last_kernel,
        [(PEERS_Y, LANES)],
        (here, got, pre, x_ref, rates, y_ref, steps),
        [ENTRY] * 2,
        name="last",
        scalars=1,
    )
    lines = swapped(lines, "gy")
    return call(return_kernel, [(ROWS, SPAN, 256)], (lines,), name="back")


def solution(mesh):
    field = P("gy", "gx", None)
    return jax.shard_map(
        body,
        mesh=mesh,
        in_specs=(field, field, P(), field, field),
        out_specs=field,
        check_vma=False,
    )
```

```python
import jax
import jax.numpy as jnp
from jax import lax
from jax.experimental import pallas as pl
from jax.experimental.pallas import tpu as pltpu
from jax.sharding import PartitionSpec as P

ROWS = 4
SPAN = 8
CELLS = ROWS * SPAN
PEERS_X = 8
PEERS_Y = 96
WIDTH = 256
LANES = 128
SLOTS = 3
PARTS = 3
USED = PARTS * CELLS
SENT = PEERS_Y * USED // LANES
TAIL = PEERS_Y - SENT

f32 = jnp.float32


def spin(value, shift, axis):
    return pltpu.roll(value, shift % value.shape[axis], axis)


def place(value, axis):
    return lax.broadcasted_iota(jnp.int32, value.shape, axis)


def strided(start, count, step):
    return pl.ds(start, count, stride=step)


def cell(conduct):
    resist = 1.0 / conduct
    one = jnp.ones_like(conduct)
    return (1.0 + resist, one, resist, one)


def joined(later, earlier):
    a2, b2, c2, k2 = later
    a1, b1, c1, k1 = earlier
    scale = 1.0 / (c2 * b1 + 1.0)
    b = (a2 * b1 + b2) * scale
    c = (c2 * a1 + c1) * scale
    k = k1 * k2 * scale
    return (k * k + b * c, b, c, k)


def kept_where(test, port):
    return tuple(jnp.where(test, m, n) for m, n in zip(port, (1.0, 0.0, 0.0, 1.0)))


def line_terms(conducts, axis, blocks, shifts):
    where = place(conducts[0], axis)
    size = conducts[0].shape[axis]
    block = cell(conducts[0])
    for conduct in conducts[1:]:
        block = joined(cell(conduct), block)
    if blocks < size:
        block = kept_where(where < blocks, block)
    front = back = block
    for s in shifts:
        earlier = kept_where(where >= s, tuple(spin(m, s, axis) for m in front))
        later = kept_where(where < size - s, tuple(spin(m, -s, axis) for m in back))
        front = joined(front, earlier)
        back = joined(later, back)
    excess = jnp.where(where == 0, 0.0, spin(front[1], 1, axis))
    behind = jnp.where(where >= blocks - 1, 0.0, spin(back[1] / back[0], -1, axis))
    ups, downs, excesses, behinds = [], [], [], []
    for conduct in conducts:
        up = conduct / (excess + conduct)
        excess = 1.0 + up * excess
        ups.append(up)
        excesses.append(excess)
    for conduct in reversed(conducts):
        down = conduct / (1.0 + behind + conduct)
        behinds.append(behind)
        downs.append(down)
        behind = down * (1.0 + behind)
    downs, behinds = downs[::-1], behinds[::-1]
    inverses = [1.0 / (e + h) for e, h in zip(excesses, behinds)]
    up_all = [ups[0]]
    for up in ups[1:]:
        up_all.append(up_all[-1] * up)
    down_all = [downs[-1]]
    for down in downs[-2::-1]:
        down_all.append(down_all[-1] * down)
    down_all = down_all[::-1]
    into_up = [m * inverse for m, inverse in zip(up_all, inverses)]
    into_down = [m * inverse for m, inverse in zip(down_all[1:] + [1.0], inverses)]
    up_s = jnp.where(where == 0, 0.0, up_all[-1])
    down_s = jnp.where(where >= blocks - 1, 0.0, down_all[0])
    steps = []
    for s in shifts:
        steps.append((up_s, down_s))
        up_s = up_s * spin(up_s, s, axis)
        down_s = down_s * spin(down_s, -s, axis)
    return ups, downs, inverses, into_up, into_down, steps


def line_solve(values, terms, axis, blocks, shifts):
    ups, downs, inverses, into_up, into_down, steps = terms
    where = place(values[0], axis)
    ahead = [values[0]]
    for value, up in zip(values[1:], ups[1:]):
        ahead.append(value + up * ahead[-1])
    back = [downs[-1] * values[-1]]
    for value, down in zip(values[-2::-1], downs[-2::-1]):
        back.append(down * (value + back[-1]))
    back = back[::-1]
    up_in, down_in = ahead[-1], back[0]
    for s, (up_s, down_s) in zip(shifts, steps):
        up_in = up_in + up_s * spin(up_in, s, axis)
        down_in = down_in + down_s * spin(down_in, -s, axis)
    up_in = jnp.where(where == 0, 0.0, spin(up_in, 1, axis))
    down_in = jnp.where(where >= blocks - 1, 0.0, spin(down_in, -1, axis))
    solved = []
    for n, value in enumerate(ahead):
        here = value + back[n + 1] if n + 1 < len(back) else value
        solved.append(here * inverses[n] + into_up[n] * up_in + into_down[n] * down_in)
    return solved


X_LINE = (1, PEERS_X, (1, 2, 4))
Y_LINE = (2, PEERS_Y, (1, 2, 4, 8, 16, 32, 64))


def turned(lists):
    return [jnp.stack([m[n] for m in lists]) for n in range(lists[0].shape[0])]


def slots(field, fill):
    low, high = field[:, :LANES], field[:, LANES:]
    lane = place(low, 1)
    rest = jnp.where(lane < 32, spin(low, 32, 1), spin(high, 64, 1))
    return low, high, jnp.where(lane < 64, rest, fill)


def mix_kernel(*refs):
    given, out, (chi, sigma, vertical, kx, ky), done = refs[:5], refs[5], refs[6:11], refs[11]
    copies = [
        pltpu.make_async_copy(source, target, done.at[n])
        for n, (source, target) in enumerate(zip(given, (chi, sigma, vertical, kx, ky)))
    ]
    for copy in copies:
        copy.start()
    for copy in copies:
        copy.wait()
    scaled = (sigma[...] * chi[...]).reshape(CELLS, WIDTH)
    blank = jnp.zeros((64, 64), f32)
    halves = []
    for h in range(2):
        weight = jnp.concatenate(
            [
                jnp.concatenate([vertical[2 * h], blank], 1),
                jnp.concatenate([blank, vertical[2 * h + 1]], 1),
            ],
            0,
        )
        halves.append(
            jnp.dot(
                scaled[:, h * LANES : (h + 1) * LANES],
                weight,
                precision=lax.Precision.HIGHEST,
                preferred_element_type=f32,
            )
        )
    mixed = jnp.concatenate(halves, 1)
    parts = [
        slots(mixed, 0.0),
        slots(kx[...].reshape(CELLS, WIDTH), 1.0),
        slots(ky[...].reshape(CELLS, WIDTH), 1.0),
    ]
    blank = jnp.zeros((CELLS, LANES), f32)
    for c in range(SLOTS):
        block = jnp.concatenate([part[c] for part in parts] + [blank], 0).T
        out[:, c * LANES : (c + 1) * LANES] = block[:PEERS_Y]


def deal_kernel(lines, out):
    blocks = []
    for c in range(SLOTS):
        block = lines[:, c * LANES : (c + 1) * LANES]
        head, tail = block[:SENT], block[SENT:]
        moved = jnp.concatenate([spin(tail, USED - n * CELLS, 1) for n in range(PARTS)], 0)
        blocks.append(jnp.where(place(head, 1) < USED, head, moved))
    for q in range(PEERS_X):
        out[q] = blocks[q % SLOTS]


def dealt(block):
    lane = place(block[:TAIL], 1)
    tail = jnp.zeros((TAIL, LANES), f32)
    for n in reversed(range(PARTS)):
        moved = spin(block[n * TAIL : (n + 1) * TAIL], n * CELLS - USED, 1)
        tail = jnp.where(lane < (n + 1) * CELLS, moved, tail)
    return jnp.concatenate([block, tail], 0)


def solve_kernel(got, out, rows):
    lane = place(jnp.zeros((LANES - PEERS_Y, LANES), f32), 1)
    spare = jnp.where(lane < CELLS, 0.0, 1.0)
    for q in range(PEERS_X):
        block = jnp.concatenate([dealt(got[q]), spare], 0).T
        rows[q * USED : (q + 1) * USED, :] = block[:USED]

    def field(n):
        return [
            [rows[strided(n * CELLS + j * SPAN + i, PEERS_X, USED), :] for j in range(ROWS)]
            for i in range(SPAN)
        ]

    u = [jnp.stack(m) for m in field(0)]
    x_terms = line_terms([jnp.stack(m) for m in field(1)], *X_LINE)
    y_terms = line_terms(turned([jnp.stack(m) for m in field(2)]), *Y_LINE)
    for _ in range(3):
        u = turned(line_solve(u, x_terms, *X_LINE))
        u = turned(line_solve(u, y_terms, *Y_LINE))
    for i in range(SPAN):
        for j in range(ROWS):
            out[strided(j * SPAN + i, PEERS_X, CELLS), :] = u[i][j]


def turn_kernel(got, out):
    blank = jnp.zeros((LANES - SLOTS * CELLS, LANES), f32)
    out[...] = jnp.concatenate([got[c] for c in range(SLOTS)] + [blank], 0).T[:PEERS_Y]


def back_kernel(lines, out):
    blank = jnp.zeros((LANES - PEERS_Y, LANES), f32)
    block = jnp.concatenate([lines[...], blank], 0).T
    low, high, rest = (block[c * CELLS : (c + 1) * CELLS] for c in range(SLOTS))
    lane = place(low, 1)
    low = jnp.where(lane < PEERS_Y, low, spin(rest, 96, 1))
    high = jnp.where(lane < PEERS_Y, high, spin(rest, 64, 1))
    out[...] = jnp.concatenate([low, high], 1).reshape(ROWS, SPAN, WIDTH)


def call(kernel, shape, args, name, scratch=(), space=pltpu.VMEM):
    return pl.pallas_call(
        kernel,
        out_shape=jax.ShapeDtypeStruct(shape, f32),
        in_specs=[pl.BlockSpec(memory_space=space)] * len(args),
        out_specs=pl.BlockSpec(memory_space=pltpu.VMEM),
        scratch_shapes=scratch,
        compiler_params=pltpu.CompilerParams(vmem_limit_bytes=16 << 20),
        name=name,
    )(*args)


def swapped(value, axis):
    return lax.all_to_all(value, axis, split_axis=0, concat_axis=0, tiled=True)


def body(chi, sigma, vertical, kx, ky):
    given = (chi, sigma, vertical, kx, ky)
    given = tuple(pltpu.with_memory_space_constraint(m, pltpu.HBM) for m in given)
    lines = call(
        mix_kernel,
        (PEERS_Y, SLOTS * LANES),
        given,
        "mix",
        [pltpu.VMEM(m.shape, f32) for m in given] + [pltpu.SemaphoreType.DMA((5,))],
        pl.ANY,
    )
    lines = swapped(lines, "gy")
    planes = call(deal_kernel, (PEERS_X, SENT, LANES), (lines,), "deal")
    planes = swapped(planes, "gx")
    planes = call(
        solve_kernel,
        (PEERS_X * CELLS, LANES),
        (planes,),
        "solve",
        [pltpu.VMEM((PEERS_X * USED, LANES), f32)],
    )
    planes = swapped(planes.reshape(PEERS_X, CELLS, LANES), "gx")
    lines = call(turn_kernel, (PEERS_Y, LANES), (planes,), "turn")
    lines = swapped(lines, "gy")
    return call(back_kernel, (ROWS, SPAN, WIDTH), (lines,), "back")


def solution(mesh):
    field = P("gy", "gx", None)
    return jax.shard_map(
        body,
        mesh=mesh,
        in_specs=(field, field, P(), field, field),
        out_specs=field,
        check_vma=False,
    )
```

```python
import jax
import jax.numpy as jnp
from jax import lax
from jax.experimental import pallas as pl
from jax.experimental.pallas import tpu as pltpu
from jax.sharding import PartitionSpec as P

ROWS = 4
SPAN = 8
CELLS = ROWS * SPAN
PEERS_X = 8
PEERS_Y = 96
WIDTH = 256
LANES = 128
SLOTS = 3
PARTS = 3
USED = PARTS * CELLS
SENT = PEERS_Y * USED // LANES
TAIL = PEERS_Y - SENT

f32 = jnp.float32


def spin(value, shift, axis):
    return pltpu.roll(value, shift % value.shape[axis], axis)


def place(value, axis):
    return lax.broadcasted_iota(jnp.int32, value.shape, axis)


def strided(start, count, step):
    return pl.ds(start, count, stride=step)


def cell(conduct):
    resist = 1.0 / conduct
    one = jnp.ones_like(conduct)
    return (1.0 + resist, one, resist, one)


def joined(later, earlier):
    a2, b2, c2, k2 = later
    a1, b1, c1, k1 = earlier
    scale = 1.0 / (c2 * b1 + 1.0)
    b = (a2 * b1 + b2) * scale
    c = (c2 * a1 + c1) * scale
    k = k1 * k2 * scale
    return (k * k + b * c, b, c, k)


def moved(members, shift, axis, test):
    return [jnp.where(test, spin(m, shift, axis), n) for m, n in members]


def ends(block, axis, shifts):
    where = place(block[0], axis)
    size = block[0].shape[axis]
    front = back = block
    for s in shifts[:-1]:
        b, c, k = moved(zip(front[1:], (0.0, 0.0, 1.0)), s, axis, where >= s)
        front = joined(front, (k * k + b * c, b, c, k))
        b, c, k = moved(zip(back[1:], (0.0, 0.0, 1.0)), -s, axis, where < size - s)
        back = joined((k * k + b * c, b, c, k), back)
    s = shifts[-1]
    a, b, c, k = front
    e, rate = moved(((b, 0.0), (k, 1.0)), s, axis, where >= s)
    scale = 1.0 / (c * e + 1.0)
    excess, passed_up = (a * e + b) * scale, k * rate * scale
    a, b, c, k = back
    scale = 1.0 / a
    h, rate = moved(((b * scale, 0.0), (k * scale, 1.0)), -s, axis, where < size - s)
    scale = 1.0 / (c * h + a)
    return excess, passed_up, (h + b) * scale, k * rate * scale


def line_terms(conducts, axis, blocks, shifts):
    where = place(conducts[0], axis)
    block = cell(conducts[0])
    for conduct in conducts[1:]:
        block = joined(cell(conduct), block)
    if blocks < conducts[0].shape[axis]:
        block = tuple(
            jnp.where(where < blocks, m, n) for m, n in zip(block, (1.0, 0.0, 0.0, 1.0))
        )
    excess, passed_up, behind, passed_down = ends(block, axis, shifts)
    excess = jnp.where(where == 0, 0.0, spin(excess, 1, axis))
    behind = jnp.where(where >= blocks - 1, 0.0, spin(behind, -1, axis))
    ups, downs, excesses, behinds = [], [], [], []
    for conduct in conducts:
        up = conduct / (excess + conduct)
        excess = 1.0 + up * excess
        ups.append(up)
        excesses.append(excess)
    for conduct in reversed(conducts):
        down = conduct / (1.0 + behind + conduct)
        behinds.append(behind)
        downs.append(down)
        behind = down * (1.0 + behind)
    downs, behinds = downs[::-1], behinds[::-1]
    inverses = [1.0 / (e + h) for e, h in zip(excesses, behinds)]
    up_all = [ups[0]]
    for up in ups[1:]:
        up_all.append(up_all[-1] * up)
    down_all = [downs[-1]]
    for down in downs[-2::-1]:
        down_all.append(down_all[-1] * down)
    down_all = down_all[::-1]
    into_up = [m * inverse for m, inverse in zip(up_all, inverses)]
    into_down = [m * inverse for m, inverse in zip(down_all[1:] + [1.0], inverses)]
    if axis == LANE:
        into_up = [m * spin(passed_up, 1, axis) for m in into_up]
        into_down = [m * spin(passed_down, -1, axis) for m in into_down]
        used = where < blocks
        steps = [jnp.where(used, 1.0 / m, 0.0) for m in (passed_up, passed_down)]
        return ups, downs, inverses, into_up, into_down, steps
    up_s = jnp.where(where == 0, 0.0, up_all[-1])
    down_s = jnp.where(where >= blocks - 1, 0.0, down_all[0])
    steps = []
    for s in shifts:
        steps.append((up_s, down_s))
        up_s = up_s * spin(up_s, s, axis)
        down_s = down_s * spin(down_s, -s, axis)
    return ups, downs, inverses, into_up, into_down, steps


def earlier_and_later():
    blank = jnp.zeros((2 * LANES, 2 * LANES), f32)
    row, column = place(blank, 0), place(blank, 1)
    ahead = jnp.where(column < LANES, column - row, row - column)
    return jnp.where(ahead > 0, 1.0, 0.0).astype(jnp.bfloat16)


def summed(ups, downs, sums):
    rows = ups.shape[0] * ups.shape[1]
    rest = jnp.concatenate([ups.reshape(rows, LANES), downs.reshape(rows, LANES)], 1)
    pieces = []
    for _ in range(3):
        pieces.append(rest.astype(jnp.bfloat16))
        rest = rest - pieces[-1].astype(f32)
    got = jnp.dot(jnp.concatenate(pieces, 0), sums, preferred_element_type=f32)
    got = got[:rows] + (got[rows : 2 * rows] + got[2 * rows :])
    return got[:, :LANES].reshape(ups.shape), got[:, LANES:].reshape(ups.shape)


def line_solve(values, terms, axis, blocks, shifts, sums=None):
    ups, downs, inverses, into_up, into_down, steps = terms
    where = place(values[0], axis)
    ahead = [values[0]]
    for value, up in zip(values[1:], ups[1:]):
        ahead.append(value + up * ahead[-1])
    back = [downs[-1] * values[-1]]
    for value, down in zip(values[-2::-1], downs[-2::-1]):
        back.append(down * (value + back[-1]))
    back = back[::-1]
    up_in, down_in = ahead[-1], back[0]
    if axis == LANE:
        up_in, down_in = summed(up_in * steps[0], down_in * steps[1], sums)
    else:
        for s, (up_s, down_s) in zip(shifts, steps):
            up_in = up_in + up_s * spin(up_in, s, axis)
            down_in = down_in + down_s * spin(down_in, -s, axis)
        up_in = jnp.where(where == 0, 0.0, spin(up_in, 1, axis))
        down_in = jnp.where(where >= blocks - 1, 0.0, spin(down_in, -1, axis))
    solved = []
    for n, value in enumerate(ahead):
        here = value + back[n + 1] if n + 1 < len(back) else value
        solved.append(here * inverses[n] + into_up[n] * up_in + into_down[n] * down_in)
    return solved


LANE = 2
X_LINE = (1, PEERS_X, (1, 2, 4))
Y_LINE = (LANE, PEERS_Y, (1, 2, 4, 8, 16, 32, 64))


def turned(lists):
    return [jnp.stack([m[n] for m in lists]) for n in range(lists[0].shape[0])]


def slots(field, fill):
    low, high = field[:, :LANES], field[:, LANES:]
    lane = place(low, 1)
    rest = jnp.where(lane < 32, spin(low, 32, 1), spin(high, 64, 1))
    return low, high, jnp.where(lane < 64, rest, fill)


def mix_kernel(*refs):
    given, out, (chi, sigma, vertical, kx, ky), done = refs[:5], refs[5], refs[6:11], refs[11]
    copies = [
        pltpu.make_async_copy(source, target, done.at[n])
        for n, (source, target) in enumerate(zip(given, (chi, sigma, vertical, kx, ky)))
    ]
    for copy in copies:
        copy.start()
    for copy in copies:
        copy.wait()
    scaled = (sigma[...] * chi[...]).reshape(CELLS, WIDTH)
    blank = jnp.zeros((64, 64), f32)
    halves = []
    for h in range(2):
        weight = jnp.concatenate(
            [
                jnp.concatenate([vertical[2 * h], blank], 1),
                jnp.concatenate([blank, vertical[2 * h + 1]], 1),
            ],
            0,
        )
        halves.append(
            jnp.dot(
                scaled[:, h * LANES : (h + 1) * LANES],
                weight,
                precision=lax.Precision.HIGHEST,
                preferred_element_type=f32,
            )
        )
    mixed = jnp.concatenate(halves, 1)
    parts = [
        slots(mixed, 0.0),
        slots(kx[...].reshape(CELLS, WIDTH), 1.0),
        slots(ky[...].reshape(CELLS, WIDTH), 1.0),
    ]
    blank = jnp.zeros((CELLS, LANES), f32)
    for c in range(SLOTS):
        block = jnp.concatenate([part[c] for part in parts] + [blank], 0).T
        out[:, c * LANES : (c + 1) * LANES] = block[:PEERS_Y]


def deal_kernel(lines, out):
    blocks = []
    for c in range(SLOTS):
        block = lines[:, c * LANES : (c + 1) * LANES]
        head, tail = block[:SENT], block[SENT:]
        moved = jnp.concatenate([spin(tail, USED - n * CELLS, 1) for n in range(PARTS)], 0)
        blocks.append(jnp.where(place(head, 1) < USED, head, moved))
    for q in range(PEERS_X):
        out[q] = blocks[q % SLOTS]


def dealt(block):
    lane = place(block[:TAIL], 1)
    tail = jnp.zeros((TAIL, LANES), f32)
    for n in reversed(range(PARTS)):
        moved = spin(block[n * TAIL : (n + 1) * TAIL], n * CELLS - USED, 1)
        tail = jnp.where(lane < (n + 1) * CELLS, moved, tail)
    return jnp.concatenate([block, tail], 0)


def solve_kernel(got, out, rows):
    lane = place(jnp.zeros((LANES - PEERS_Y, LANES), f32), 1)
    spare = jnp.where(lane < CELLS, 0.0, 1.0)
    for q in range(PEERS_X):
        block = jnp.concatenate([dealt(got[q]), spare], 0).T
        for n in range(PARTS * ROWS):
            rows[strided(n * SPAN * PEERS_X + q, SPAN, PEERS_X), :] = block[n * SPAN : (n + 1) * SPAN]

    def field(n):
        at = [[((n * ROWS + j) * SPAN + i) * PEERS_X for j in range(ROWS)] for i in range(SPAN)]
        return [[rows[m : m + PEERS_X, :] for m in some] for some in at]

    sums = earlier_and_later()
    u = [jnp.stack(m) for m in field(0)]
    x_terms = line_terms([jnp.stack(m) for m in field(1)], *X_LINE)
    y_terms = line_terms(turned([jnp.stack(m) for m in field(2)]), *Y_LINE)
    for _ in range(3):
        u = turned(line_solve(u, x_terms, *X_LINE))
        u = turned(line_solve(u, y_terms, *Y_LINE, sums))
    for i in range(SPAN):
        for j in range(ROWS):
            at = (j * SPAN + i) * PEERS_X
            rows[at : at + PEERS_X, :] = u[i][j]
    for q in range(PEERS_X):
        for j in range(ROWS):
            at = q * CELLS + j * SPAN
            out[at : at + SPAN, :] = rows[strided(j * SPAN * PEERS_X + q, SPAN, PEERS_X), :]


def turn_kernel(got, out):
    blank = jnp.zeros((LANES - SLOTS * CELLS, LANES), f32)
    out[...] = jnp.concatenate([got[c] for c in range(SLOTS)] + [blank], 0).T[:PEERS_Y]


def back_kernel(lines, out):
    blank = jnp.zeros((LANES - PEERS_Y, LANES), f32)
    block = jnp.concatenate([lines[...], blank], 0).T
    low, high, rest = (block[c * CELLS : (c + 1) * CELLS] for c in range(SLOTS))
    lane = place(low, 1)
    low = jnp.where(lane < PEERS_Y, low, spin(rest, 96, 1))
    high = jnp.where(lane < PEERS_Y, high, spin(rest, 64, 1))
    out[...] = jnp.concatenate([low, high], 1).reshape(ROWS, SPAN, WIDTH)


def call(kernel, shape, args, name, scratch=(), space=pltpu.VMEM):
    return pl.pallas_call(
        kernel,
        out_shape=jax.ShapeDtypeStruct(shape, f32),
        in_specs=[pl.BlockSpec(memory_space=space)] * len(args),
        out_specs=pl.BlockSpec(memory_space=pltpu.VMEM),
        scratch_shapes=scratch,
        compiler_params=pltpu.CompilerParams(vmem_limit_bytes=16 << 20),
        name=name,
    )(*args)


def swapped(value, axis):
    return lax.all_to_all(value, axis, split_axis=0, concat_axis=0, tiled=True)


def body(chi, sigma, vertical, kx, ky):
    given = (chi, sigma, vertical, kx, ky)
    given = tuple(pltpu.with_memory_space_constraint(m, pltpu.HBM) for m in given)
    lines = call(
        mix_kernel,
        (PEERS_Y, SLOTS * LANES),
        given,
        "mix",
        [pltpu.VMEM(m.shape, f32) for m in given] + [pltpu.SemaphoreType.DMA((5,))],
        pl.ANY,
    )
    lines = swapped(lines, "gy")
    planes = call(deal_kernel, (PEERS_X, SENT, LANES), (lines,), "deal")
    planes = swapped(planes, "gx")
    planes = call(
        solve_kernel,
        (PEERS_X * CELLS, LANES),
        (planes,),
        "solve",
        [pltpu.VMEM((PEERS_X * USED, LANES), f32)],
    )
    planes = swapped(planes.reshape(PEERS_X, CELLS, LANES), "gx")
    lines = call(turn_kernel, (PEERS_Y, LANES), (planes,), "turn")
    lines = swapped(lines, "gy")
    return call(back_kernel, (ROWS, SPAN, WIDTH), (lines,), "back")


def solution(mesh):
    field = P("gy", "gx", None)
    return jax.shard_map(
        body,
        mesh=mesh,
        in_specs=(field, field, P(), field, field),
        out_specs=field,
        check_vma=False,
    )
```

```python
import jax
import jax.numpy as jnp
from jax import lax
from jax.experimental import pallas as pl
from jax.experimental.pallas import tpu as pltpu
from jax.sharding import PartitionSpec as P

ROWS = 4
SPAN = 8
CELLS = ROWS * SPAN
PEERS_X = 8
PEERS_Y = 96
WIDTH = 256
LANES = 128
SLOTS = 3
PARTS = 3
USED = PARTS * CELLS
SENT = PEERS_Y * USED // LANES
TAIL = PEERS_Y - SENT

f32 = jnp.float32


def spin(value, shift, axis):
    return pltpu.roll(value, shift % value.shape[axis], axis)


def place(value, axis):
    return lax.broadcasted_iota(jnp.int32, value.shape, axis)


def strided(start, count, step):
    return pl.ds(start, count, stride=step)


def cell(conduct):
    resist = 1.0 / conduct
    one = jnp.ones_like(conduct)
    return (1.0 + resist, one, resist, one)


def joined(later, earlier):
    a2, b2, c2, k2 = later
    a1, b1, c1, k1 = earlier
    scale = 1.0 / (c2 * b1 + 1.0)
    b = (a2 * b1 + b2) * scale
    c = (c2 * a1 + c1) * scale
    k = k1 * k2 * scale
    return (k * k + b * c, b, c, k)


def moved(members, shift, axis, test):
    return [jnp.where(test, spin(m, shift, axis), n) for m, n in members]


def ends(block, axis, shifts):
    where = place(block[0], axis)
    size = block[0].shape[axis]
    front = back = block
    for s in shifts[:-1]:
        b, c, k = moved(zip(front[1:], (0.0, 0.0, 1.0)), s, axis, where >= s)
        front = joined(front, (k * k + b * c, b, c, k))
        b, c, k = moved(zip(back[1:], (0.0, 0.0, 1.0)), -s, axis, where < size - s)
        back = joined((k * k + b * c, b, c, k), back)
    s = shifts[-1]
    a, b, c, k = front
    e, rate = moved(((b, 0.0), (k, 1.0)), s, axis, where >= s)
    scale = 1.0 / (c * e + 1.0)
    excess, passed_up = (a * e + b) * scale, k * rate * scale
    a, b, c, k = back
    scale = 1.0 / a
    h, rate = moved(((b * scale, 0.0), (k * scale, 1.0)), -s, axis, where < size - s)
    scale = 1.0 / (c * h + a)
    return excess, passed_up, (h + b) * scale, k * rate * scale


def line_terms(conducts, axis, blocks, shifts):
    where = place(conducts[0], axis)
    block = cell(conducts[0])
    for conduct in conducts[1:]:
        block = joined(cell(conduct), block)
    if blocks < conducts[0].shape[axis]:
        block = tuple(
            jnp.where(where < blocks, m, n) for m, n in zip(block, (1.0, 0.0, 0.0, 1.0))
        )
    excess, passed_up, behind, passed_down = ends(block, axis, shifts)
    excess = jnp.where(where == 0, 0.0, spin(excess, 1, axis))
    behind = jnp.where(where >= blocks - 1, 0.0, spin(behind, -1, axis))
    ups, downs, excesses, behinds = [], [], [], []
    for conduct in conducts:
        up = conduct / (excess + conduct)
        excess = 1.0 + up * excess
        ups.append(up)
        excesses.append(excess)
    for conduct in reversed(conducts):
        down = conduct / (1.0 + behind + conduct)
        behinds.append(behind)
        downs.append(down)
        behind = down * (1.0 + behind)
    downs, behinds = downs[::-1], behinds[::-1]
    inverses = [1.0 / (e + h) for e, h in zip(excesses, behinds)]
    up_all = [ups[0]]
    for up in ups[1:]:
        up_all.append(up_all[-1] * up)
    down_all = [downs[-1]]
    for down in downs[-2::-1]:
        down_all.append(down_all[-1] * down)
    down_all = down_all[::-1]
    into_up = [m * inverse for m, inverse in zip(up_all, inverses)]
    into_down = [m * inverse for m, inverse in zip(down_all[1:] + [1.0], inverses)]
    if axis == LANE:
        into_up = [m * spin(passed_up, 1, axis) for m in into_up]
        into_down = [m * spin(passed_down, -1, axis) for m in into_down]
        used = where < blocks
        steps = [jnp.where(used, 1.0 / m, 0.0) for m in (passed_up, passed_down)]
        return ups, downs, inverses, into_up, into_down, steps
    up_s = jnp.where(where == 0, 0.0, up_all[-1])
    down_s = jnp.where(where >= blocks - 1, 0.0, down_all[0])
    steps = []
    for s in shifts:
        steps.append((up_s, down_s))
        up_s = up_s * spin(up_s, s, axis)
        down_s = down_s * spin(down_s, -s, axis)
    return ups, downs, inverses, into_up, into_down, steps


def earlier_and_later():
    blank = jnp.zeros((2 * LANES, 2 * LANES), f32)
    row, column = place(blank, 0), place(blank, 1)
    ahead = jnp.where(column < LANES, column - row, row - column)
    return jnp.where(ahead > 0, 1.0, 0.0).astype(jnp.bfloat16)


def summed(ups, downs, sums):
    rows = ups.shape[0] * ups.shape[1]
    rest = jnp.concatenate([ups.reshape(rows, LANES), downs.reshape(rows, LANES)], 1)
    pieces = []
    for _ in range(3):
        pieces.append(rest.astype(jnp.bfloat16))
        rest = rest - pieces[-1].astype(f32)
    got = jnp.dot(jnp.concatenate(pieces, 0), sums, preferred_element_type=f32)
    got = got[:rows] + (got[rows : 2 * rows] + got[2 * rows :])
    return got[:, :LANES].reshape(ups.shape), got[:, LANES:].reshape(ups.shape)


def line_solve(values, terms, axis, blocks, shifts, sums=None):
    ups, downs, inverses, into_up, into_down, steps = terms
    where = place(values[0], axis)
    ahead = [values[0]]
    for value, up in zip(values[1:], ups[1:]):
        ahead.append(value + up * ahead[-1])
    back = [downs[-1] * values[-1]]
    for value, down in zip(values[-2::-1], downs[-2::-1]):
        back.append(down * (value + back[-1]))
    back = back[::-1]
    up_in, down_in = ahead[-1], back[0]
    if axis == LANE:
        up_in, down_in = summed(up_in * steps[0], down_in * steps[1], sums)
    else:
        for s, (up_s, down_s) in zip(shifts, steps):
            up_in = up_in + up_s * spin(up_in, s, axis)
            down_in = down_in + down_s * spin(down_in, -s, axis)
        up_in = jnp.where(where == 0, 0.0, spin(up_in, 1, axis))
        down_in = jnp.where(where >= blocks - 1, 0.0, spin(down_in, -1, axis))
    solved = []
    for n, value in enumerate(ahead):
        here = value + back[n + 1] if n + 1 < len(back) else value
        solved.append(here * inverses[n] + into_up[n] * up_in + into_down[n] * down_in)
    return solved


LANE = 2
X_LINE = (1, PEERS_X, (1, 2, 4))
Y_LINE = (LANE, PEERS_Y, (1, 2, 4, 8, 16, 32, 64))


def turned(lists):
    return [jnp.stack([m[n] for m in lists]) for n in range(lists[0].shape[0])]


def slots(field, fill):
    low, high = field[:, :LANES], field[:, LANES:]
    lane = place(low, 1)
    rest = jnp.where(lane < 32, spin(low, 32, 1), spin(high, 64, 1))
    return low, high, jnp.where(lane < 64, rest, fill)


def mix_kernel(*refs):
    given, out, (chi, sigma, vertical, kx, ky), done = refs[:5], refs[5], refs[6:11], refs[11]
    copies = [
        pltpu.make_async_copy(source, target, done.at[n])
        for n, (source, target) in enumerate(zip(given, (chi, sigma, vertical, kx, ky)))
    ]
    for n in (2, 0, 1, 3, 4):
        copies[n].start()
    for copy in copies:
        copy.wait()
    scaled = (sigma[...] * chi[...]).reshape(CELLS, WIDTH)
    blank = jnp.zeros((64, 64), f32)
    halves = []
    for h in range(2):
        weight = jnp.concatenate(
            [
                jnp.concatenate([vertical[2 * h], blank], 1),
                jnp.concatenate([blank, vertical[2 * h + 1]], 1),
            ],
            0,
        )
        halves.append(
            jnp.dot(
                scaled[:, h * LANES : (h + 1) * LANES],
                weight,
                precision=lax.Precision.HIGHEST,
                preferred_element_type=f32,
            )
        )
    mixed = jnp.concatenate(halves, 1)
    parts = [
        slots(mixed, 0.0),
        slots(kx[...].reshape(CELLS, WIDTH), 1.0),
        slots(ky[...].reshape(CELLS, WIDTH), 1.0),
    ]
    blank = jnp.zeros((CELLS, LANES), f32)
    for c in range(SLOTS):
        block = jnp.concatenate([part[c] for part in parts] + [blank], 0).T
        out[strided(c, PEERS_Y, SLOTS), :] = block[:PEERS_Y]


def deal_kernel(lines, out):
    blocks = []
    for c in range(SLOTS):
        block = lines[strided(c, PEERS_Y, SLOTS), :]
        head, tail = block[:SENT], block[SENT:]
        moved = jnp.concatenate([spin(tail, USED - n * CELLS, 1) for n in range(PARTS)], 0)
        blocks.append(jnp.where(place(head, 1) < USED, head, moved))
    for q in range(PEERS_X):
        out[q] = blocks[q % SLOTS]


def dealt(block):
    lane = place(block[:TAIL], 1)
    tail = jnp.zeros((TAIL, LANES), f32)
    for n in reversed(range(PARTS)):
        moved = spin(block[n * TAIL : (n + 1) * TAIL], n * CELLS - USED, 1)
        tail = jnp.where(lane < (n + 1) * CELLS, moved, tail)
    return jnp.concatenate([block, tail], 0)


def solve_kernel(got, out, rows):
    lane = place(jnp.zeros((LANES - PEERS_Y, LANES), f32), 1)
    spare = jnp.where(lane < CELLS, 0.0, 1.0)
    for q in range(PEERS_X):
        block = jnp.concatenate([dealt(got[q]), spare], 0).T
        for n in range(PARTS * ROWS):
            rows[strided(n * SPAN * PEERS_X + q, SPAN, PEERS_X), :] = block[n * SPAN : (n + 1) * SPAN]

    def field(n):
        at = [[((n * ROWS + j) * SPAN + i) * PEERS_X for j in range(ROWS)] for i in range(SPAN)]
        return [[rows[m : m + PEERS_X, :] for m in some] for some in at]

    sums = earlier_and_later()
    u = [jnp.stack(m) for m in field(0)]
    x_terms = line_terms([jnp.stack(m) for m in field(1)], *X_LINE)
    y_terms = line_terms(turned([jnp.stack(m) for m in field(2)]), *Y_LINE)
    for _ in range(3):
        u = turned(line_solve(u, x_terms, *X_LINE))
        u = turned(line_solve(u, y_terms, *Y_LINE, sums))
    for i in range(SPAN):
        for j in range(ROWS):
            at = (j * SPAN + i) * PEERS_X
            rows[at : at + PEERS_X, :] = u[i][j]
    lane = place(u[0][0], 1)
    for q in range(PEERS_X):
        *head, tail = (rows[strided(j * SPAN * PEERS_X + q, SPAN, PEERS_X), :] for j in range(ROWS))
        for j, value in enumerate(head):
            moved = spin(tail, USED - j * CELLS, 1)
            out[q, j * SPAN : (j + 1) * SPAN, :] = jnp.where(lane < USED, value, moved)


def turn_kernel(got, out):
    blank = jnp.zeros((LANES - SLOTS * CELLS, LANES), f32)
    lane = place(jnp.zeros((SPAN, LANES), f32), 1)
    blocks = []
    for c in range(SLOTS):
        tail = jnp.zeros((SPAN, LANES), f32)
        for j in reversed(range(PARTS)):
            moved = spin(got[c, j * SPAN : (j + 1) * SPAN, :], j * CELLS - USED, 1)
            tail = jnp.where(lane < (j + 1) * CELLS, moved, tail)
        blocks += [got[c], tail]
    out[...] = jnp.concatenate(blocks + [blank], 0).T[:PEERS_Y]


def back_kernel(lines, out):
    blank = jnp.zeros((LANES - PEERS_Y, LANES), f32)
    block = jnp.concatenate([lines[...], blank], 0).T
    low, high, rest = (block[c * CELLS : (c + 1) * CELLS] for c in range(SLOTS))
    lane = place(low, 1)
    low = jnp.where(lane < PEERS_Y, low, spin(rest, 96, 1))
    high = jnp.where(lane < PEERS_Y, high, spin(rest, 64, 1))
    out[...] = jnp.concatenate([low, high], 1).reshape(ROWS, SPAN, WIDTH)


def call(kernel, shape, args, name, scratch=(), space=pltpu.VMEM):
    return pl.pallas_call(
        kernel,
        out_shape=jax.ShapeDtypeStruct(shape, f32),
        in_specs=[pl.BlockSpec(memory_space=space)] * len(args),
        out_specs=pl.BlockSpec(memory_space=pltpu.VMEM),
        scratch_shapes=scratch,
        compiler_params=pltpu.CompilerParams(vmem_limit_bytes=16 << 20),
        name=name,
    )(*args)


def swapped(value, axis):
    return lax.all_to_all(value, axis, split_axis=0, concat_axis=0, tiled=True)


def body(chi, sigma, vertical, kx, ky):
    given = (chi, sigma, vertical, kx, ky)
    given = tuple(pltpu.with_memory_space_constraint(m, pltpu.HBM) for m in given)
    lines = call(
        mix_kernel,
        (PEERS_Y * SLOTS, LANES),
        given,
        "mix",
        [pltpu.VMEM(m.shape, f32) for m in given] + [pltpu.SemaphoreType.DMA((5,))],
        pl.ANY,
    )
    lines = swapped(lines.reshape(PEERS_Y, 1, SLOTS * LANES), "gy").reshape(lines.shape)
    planes = call(deal_kernel, (PEERS_X, SENT, LANES), (lines,), "deal")
    planes = swapped(planes, "gx")
    planes = call(
        solve_kernel,
        (PEERS_X, CELLS - SPAN, LANES),
        (planes,),
        "solve",
        [pltpu.VMEM((PEERS_X * USED, LANES), f32)],
    )
    planes = swapped(planes, "gx")
    lines = call(turn_kernel, (PEERS_Y, LANES), (planes,), "turn")
    lines = swapped(lines, "gy")
    return call(back_kernel, (ROWS, SPAN, WIDTH), (lines,), "back")


def solution(mesh):
    field = P("gy", "gx", None)
    return jax.shard_map(
        body,
        mesh=mesh,
        in_specs=(field, field, P(), field, field),
        out_specs=field,
        check_vma=False,
    )
```

```python
import jax
import jax.numpy as jnp
from jax import lax
from jax.experimental import pallas as pl
from jax.experimental.pallas import tpu as pltpu
from jax.sharding import PartitionSpec as P

ROWS = 4
SPAN = 8
CELLS = ROWS * SPAN
PEERS_X = 8
PEERS_Y = 96
WIDTH = 256
LANES = 128
SLOTS = 3
PARTS = 3
USED = PARTS * CELLS
SENT = PEERS_Y * USED // LANES
TAIL = PEERS_Y - SENT

f32 = jnp.float32


def spin(value, shift, axis):
    return pltpu.roll(value, shift % value.shape[axis], axis)


def place(value, axis):
    return lax.broadcasted_iota(jnp.int32, value.shape, axis)


def strided(start, count, step):
    return pl.ds(start, count, stride=step)


def cell(conduct):
    resist = 1.0 / conduct
    one = jnp.ones_like(conduct)
    return (1.0 + resist, one, resist, one)


def joined(later, earlier):
    a2, b2, c2, k2 = later
    a1, b1, c1, k1 = earlier
    scale = 1.0 / (c2 * b1 + 1.0)
    b = (a2 * b1 + b2) * scale
    c = (c2 * a1 + c1) * scale
    k = k1 * k2 * scale
    return (k * k + b * c, b, c, k)


def moved(members, shift, axis, test):
    return [jnp.where(test, spin(m, shift, axis), n) for m, n in members]


def ends(block, axis, shifts):
    where = place(block[0], axis)
    size = block[0].shape[axis]
    front = back = block
    for s in shifts[:-1]:
        b, c, k = moved(zip(front[1:], (0.0, 0.0, 1.0)), s, axis, where >= s)
        front = joined(front, (k * k + b * c, b, c, k))
        b, c, k = moved(zip(back[1:], (0.0, 0.0, 1.0)), -s, axis, where < size - s)
        back = joined((k * k + b * c, b, c, k), back)
    s = shifts[-1]
    a, b, c, k = front
    e, rate = moved(((b, 0.0), (k, 1.0)), s, axis, where >= s)
    scale = 1.0 / (c * e + 1.0)
    excess, passed_up = (a * e + b) * scale, k * rate * scale
    a, b, c, k = back
    scale = 1.0 / a
    h, rate = moved(((b * scale, 0.0), (k * scale, 1.0)), -s, axis, where < size - s)
    scale = 1.0 / (c * h + a)
    return excess, passed_up, (h + b) * scale, k * rate * scale


def line_terms(conducts, axis, blocks, shifts):
    where = place(conducts[0], axis)
    block = cell(conducts[0])
    for conduct in conducts[1:]:
        block = joined(cell(conduct), block)
    if blocks < conducts[0].shape[axis]:
        block = tuple(
            jnp.where(where < blocks, m, n) for m, n in zip(block, (1.0, 0.0, 0.0, 1.0))
        )
    excess, passed_up, behind, passed_down = ends(block, axis, shifts)
    excess = jnp.where(where == 0, 0.0, spin(excess, 1, axis))
    behind = jnp.where(where >= blocks - 1, 0.0, spin(behind, -1, axis))
    ups, downs, excesses, behinds = [], [], [], []
    for conduct in conducts:
        up = conduct / (excess + conduct)
        excess = 1.0 + up * excess
        ups.append(up)
        excesses.append(excess)
    for conduct in reversed(conducts):
        down = conduct / (1.0 + behind + conduct)
        behinds.append(behind)
        downs.append(down)
        behind = down * (1.0 + behind)
    downs, behinds = downs[::-1], behinds[::-1]
    inverses = [1.0 / (e + h) for e, h in zip(excesses, behinds)]
    up_all = [ups[0]]
    for up in ups[1:]:
        up_all.append(up_all[-1] * up)
    down_all = [downs[-1]]
    for down in downs[-2::-1]:
        down_all.append(down_all[-1] * down)
    down_all = down_all[::-1]
    into_up = [m * inverse for m, inverse in zip(up_all, inverses)]
    into_down = [m * inverse for m, inverse in zip(down_all[1:] + [1.0], inverses)]
    if axis == LANE:
        into_up = [m * spin(passed_up, 1, axis) for m in into_up]
        into_down = [m * spin(passed_down, -1, axis) for m in into_down]
        used = where < blocks
        steps = [jnp.where(used, 1.0 / m, 0.0) for m in (passed_up, passed_down)]
        return ups, downs, inverses, into_up, into_down, steps
    up_s = jnp.where(where == 0, 0.0, up_all[-1])
    down_s = jnp.where(where >= blocks - 1, 0.0, down_all[0])
    steps = []
    for s in shifts:
        steps.append((up_s, down_s))
        up_s = up_s * spin(up_s, s, axis)
        down_s = down_s * spin(down_s, -s, axis)
    return ups, downs, inverses, into_up, into_down, steps


def earlier_and_later():
    blank = jnp.zeros((2 * LANES, 2 * LANES), f32)
    row, column = place(blank, 0), place(blank, 1)
    ahead = jnp.where(column < LANES, column - row, row - column)
    return jnp.where(ahead > 0, 1.0, 0.0).astype(jnp.bfloat16)


def summed(ups, downs, sums):
    rows = ups.shape[0] * ups.shape[1]
    rest = jnp.concatenate([ups.reshape(rows, LANES), downs.reshape(rows, LANES)], 1)
    pieces = []
    for _ in range(3):
        pieces.append(rest.astype(jnp.bfloat16))
        rest = rest - pieces[-1].astype(f32)
    got = jnp.dot(jnp.concatenate(pieces, 0), sums, preferred_element_type=f32)
    got = got[:rows] + (got[rows : 2 * rows] + got[2 * rows :])
    return got[:, :LANES].reshape(ups.shape), got[:, LANES:].reshape(ups.shape)


def line_solve(values, terms, axis, blocks, shifts, sums=None):
    ups, downs, inverses, into_up, into_down, steps = terms
    where = place(values[0], axis)
    ahead = [values[0]]
    for value, up in zip(values[1:], ups[1:]):
        ahead.append(value + up * ahead[-1])
    back = [downs[-1] * values[-1]]
    for value, down in zip(values[-2::-1], downs[-2::-1]):
        back.append(down * (value + back[-1]))
    back = back[::-1]
    up_in, down_in = ahead[-1], back[0]
    if axis == LANE:
        up_in, down_in = summed(up_in * steps[0], down_in * steps[1], sums)
    else:
        for s, (up_s, down_s) in zip(shifts, steps):
            up_in = up_in + up_s * spin(up_in, s, axis)
            down_in = down_in + down_s * spin(down_in, -s, axis)
        up_in = jnp.where(where == 0, 0.0, spin(up_in, 1, axis))
        down_in = jnp.where(where >= blocks - 1, 0.0, spin(down_in, -1, axis))
    solved = []
    for n, value in enumerate(ahead):
        here = value + back[n + 1] if n + 1 < len(back) else value
        solved.append(here * inverses[n] + into_up[n] * up_in + into_down[n] * down_in)
    return solved


LANE = 2
X_LINE = (1, PEERS_X, (1, 2, 4))
Y_LINE = (LANE, PEERS_Y, (1, 2, 4, 8, 16, 32, 64))


def turned(lists):
    return [jnp.stack([m[n] for m in lists]) for n in range(lists[0].shape[0])]


def slots(field, fill):
    low, high = field[:, :LANES], field[:, LANES:]
    lane = place(low, 1)
    rest = jnp.where(lane < 32, spin(low, 32, 1), spin(high, 64, 1))
    return low, high, jnp.where(lane < 64, rest, fill)


def mix_kernel(*refs):
    given, out, (chi, sigma, vertical, kx, ky), done = refs[:5], refs[5], refs[6:11], refs[11]
    copies = [
        pltpu.make_async_copy(source, target, done.at[n])
        for n, (source, target) in enumerate(zip(given, (chi, sigma, vertical, kx, ky)))
    ]
    for n in (2, 0, 1, 3, 4):
        copies[n].start()
    for copy in copies[:3]:
        copy.wait()
    scaled = (sigma[...] * chi[...]).reshape(CELLS, WIDTH)
    blank = jnp.zeros((64, 64), f32)
    halves = []
    for h in range(2):
        weight = jnp.concatenate(
            [
                jnp.concatenate([vertical[2 * h], blank], 1),
                jnp.concatenate([blank, vertical[2 * h + 1]], 1),
            ],
            0,
        )
        halves.append(
            jnp.dot(
                scaled[:, h * LANES : (h + 1) * LANES],
                weight,
                precision=lax.Precision.HIGHEST,
                preferred_element_type=f32,
            )
        )
    mixed = jnp.concatenate(halves, 1)
    for copy in copies[3:]:
        copy.wait()
    parts = [
        slots(mixed, 0.0),
        slots(kx[...].reshape(CELLS, WIDTH), 1.0),
        slots(ky[...].reshape(CELLS, WIDTH), 1.0),
    ]
    blank = jnp.zeros((CELLS, LANES), f32)
    for c in range(SLOTS):
        block = jnp.concatenate([part[c] for part in parts] + [blank], 0).T
        out[strided(c, PEERS_Y, SLOTS), :] = block[:PEERS_Y]


def deal_kernel(lines, out):
    spare = jnp.zeros((LANES - PEERS_Y, LANES), f32)
    blocks = []
    for c in range(SLOTS):
        block = jnp.concatenate([lines[strided(c, PEERS_Y, SLOTS), :], spare], 0).T[:USED]
        head, tail = block[:SENT], block[SENT:]
        moved = jnp.concatenate([spin(tail, USED - n * CELLS, 1) for n in range(PARTS)], 0)
        blocks.append(jnp.where(place(head, 1) < USED, head, moved))
    for q in range(PEERS_X):
        out[q] = blocks[q % SLOTS]


def dealt(block):
    lane = place(block[:TAIL], 1)
    tail = jnp.zeros((TAIL, LANES), f32)
    for n in reversed(range(PARTS)):
        moved = spin(block[n * TAIL : (n + 1) * TAIL], n * CELLS - USED, 1)
        tail = jnp.where(lane < (n + 1) * CELLS, moved, tail)
    return jnp.concatenate([block, tail], 0)


def solve_kernel(got, out, rows):
    for q in range(PEERS_X):
        block = dealt(got[q])
        for n in range(PARTS * ROWS):
            rows[strided(n * SPAN * PEERS_X + q, SPAN, PEERS_X), :] = block[n * SPAN : (n + 1) * SPAN]

    def field(n):
        at = [[((n * ROWS + j) * SPAN + i) * PEERS_X for j in range(ROWS)] for i in range(SPAN)]
        return [[rows[m : m + PEERS_X, :] for m in some] for some in at]

    sums = earlier_and_later()
    u = [jnp.stack(m) for m in field(0)]
    x_terms = line_terms([jnp.stack(m) for m in field(1)], *X_LINE)
    y_terms = line_terms(turned([jnp.stack(m) for m in field(2)]), *Y_LINE)
    for _ in range(3):
        u = turned(line_solve(u, x_terms, *X_LINE))
        u = turned(line_solve(u, y_terms, *Y_LINE, sums))
    for i in range(SPAN):
        for j in range(ROWS):
            at = (j * SPAN + i) * PEERS_X
            rows[at : at + PEERS_X, :] = u[i][j]
    lane = place(u[0][0], 1)
    for q in range(PEERS_X):
        *head, tail = (rows[strided(j * SPAN * PEERS_X + q, SPAN, PEERS_X), :] for j in range(ROWS))
        for j, value in enumerate(head):
            moved = spin(tail, USED - j * CELLS, 1)
            out[q, j * SPAN : (j + 1) * SPAN, :] = jnp.where(lane < USED, value, moved)


def turn_kernel(got, out):
    blank = jnp.zeros((LANES - SLOTS * CELLS, LANES), f32)
    lane = place(jnp.zeros((SPAN, LANES), f32), 1)
    blocks = []
    for c in range(SLOTS):
        tail = jnp.zeros((SPAN, LANES), f32)
        for j in reversed(range(PARTS)):
            moved = spin(got[c, j * SPAN : (j + 1) * SPAN, :], j * CELLS - USED, 1)
            tail = jnp.where(lane < (j + 1) * CELLS, moved, tail)
        blocks += [got[c], tail]
    out[...] = jnp.concatenate(blocks + [blank], 0).T[:PEERS_Y]


def back_kernel(lines, out):
    blank = jnp.zeros((LANES - PEERS_Y, LANES), f32)
    block = jnp.concatenate([lines[...], blank], 0).T
    low, high, rest = (block[c * CELLS : (c + 1) * CELLS] for c in range(SLOTS))
    lane = place(low, 1)
    low = jnp.where(lane < PEERS_Y, low, spin(rest, 96, 1))
    high = jnp.where(lane < PEERS_Y, high, spin(rest, 64, 1))
    out[...] = jnp.concatenate([low, high], 1).reshape(ROWS, SPAN, WIDTH)


def call(kernel, shape, args, name, scratch=(), space=pltpu.VMEM):
    return pl.pallas_call(
        kernel,
        out_shape=jax.ShapeDtypeStruct(shape, f32),
        in_specs=[pl.BlockSpec(memory_space=space)] * len(args),
        out_specs=pl.BlockSpec(memory_space=pltpu.VMEM),
        scratch_shapes=scratch,
        compiler_params=pltpu.CompilerParams(vmem_limit_bytes=16 << 20),
        name=name,
    )(*args)


def swapped(value, axis):
    return lax.all_to_all(value, axis, split_axis=0, concat_axis=0, tiled=True)


def body(chi, sigma, vertical, kx, ky):
    given = (chi, sigma, vertical, kx, ky)
    given = tuple(pltpu.with_memory_space_constraint(m, pltpu.HBM) for m in given)
    lines = call(
        mix_kernel,
        (PEERS_Y * SLOTS, LANES),
        given,
        "mix",
        [pltpu.VMEM(m.shape, f32) for m in given] + [pltpu.SemaphoreType.DMA((5,))],
        pl.ANY,
    )
    lines = swapped(lines.reshape(PEERS_Y, 1, SLOTS * LANES), "gy").reshape(lines.shape)
    planes = call(deal_kernel, (PEERS_X, SENT, LANES), (lines,), "deal")
    planes = swapped(planes, "gx")
    planes = call(
        solve_kernel,
        (PEERS_X, CELLS - SPAN, LANES),
        (planes,),
        "solve",
        [pltpu.VMEM((PEERS_X * USED, LANES), f32)],
    )
    planes = swapped(planes, "gx")
    lines = call(turn_kernel, (PEERS_Y, LANES), (planes,), "turn")
    lines = swapped(lines, "gy")
    return call(back_kernel, (ROWS, SPAN, WIDTH), (lines,), "back")


def solution(mesh):
    field = P("gy", "gx", None)
    return jax.shard_map(
        body,
        mesh=mesh,
        in_specs=(field, field, P(), field, field),
        out_specs=field,
        check_vma=False,
    )
```

```python
import jax
import jax.numpy as jnp
from jax import lax
from jax.experimental import pallas as pl
from jax.experimental.pallas import tpu as pltpu
from jax.sharding import PartitionSpec as P

ROWS = 4
SPAN = 8
CELLS = ROWS * SPAN
PEERS_X = 8
PEERS_Y = 96
WIDTH = 256
LANES = 128
SLOTS = 3
PARTS = 3
USED = PARTS * CELLS
SENT = PEERS_Y * USED // LANES
TAIL = PEERS_Y - SENT

f32 = jnp.float32


def spin(value, shift, axis):
    return pltpu.roll(value, shift % value.shape[axis], axis)


def place(value, axis):
    return lax.broadcasted_iota(jnp.int32, value.shape, axis)


def strided(start, count, step):
    return pl.ds(start, count, stride=step)


def cell(conduct):
    resist = 1.0 / conduct
    one = jnp.ones_like(conduct)
    return (1.0 + resist, one, resist, one)


def lengthened(conduct, earlier):
    a, b, c, k = earlier
    scale = 1.0 / (b + conduct)
    share = conduct * scale
    b, c, k = 1.0 + share * b, a * scale + share * c, share * k
    return (k * k + b * c, b, c, k)


def joined(later, earlier):
    a2, b2, c2, k2 = later
    a1, b1, c1, k1 = earlier
    scale = 1.0 / (c2 * b1 + 1.0)
    b = (a2 * b1 + b2) * scale
    c = (c2 * a1 + c1) * scale
    k = k1 * k2 * scale
    return (k * k + b * c, b, c, k)


def moved(members, shift, axis, test):
    return [jnp.where(test, spin(m, shift, axis), n) for m, n in members]


def ends(block, axis, shifts):
    where = place(block[0], axis)
    size = block[0].shape[axis]
    front = back = block
    for s in shifts[:-1]:
        b, c, k = moved(zip(front[1:], (0.0, 0.0, 1.0)), s, axis, where >= s)
        front = joined(front, (k * k + b * c, b, c, k))
        b, c, k = moved(zip(back[1:], (0.0, 0.0, 1.0)), -s, axis, where < size - s)
        back = joined((k * k + b * c, b, c, k), back)
    s = shifts[-1]
    a, b, c, k = front
    e, rate = moved(((b, 0.0), (k, 1.0)), s, axis, where >= s)
    scale = 1.0 / (c * e + 1.0)
    excess, passed_up = (a * e + b) * scale, k * rate * scale
    a, b, c, k = back
    scale = 1.0 / a
    h, rate = moved(((b * scale, 0.0), (k * scale, 1.0)), -s, axis, where < size - s)
    scale = 1.0 / (c * h + a)
    return excess, passed_up, (h + b) * scale, k * rate * scale


def line_terms(conducts, axis, blocks, shifts):
    where = place(conducts[0], axis)
    block = cell(conducts[0])
    for conduct in conducts[1:]:
        block = lengthened(conduct, block)
    if blocks < conducts[0].shape[axis]:
        block = tuple(
            jnp.where(where < blocks, m, n) for m, n in zip(block, (1.0, 0.0, 0.0, 1.0))
        )
    excess, passed_up, behind, passed_down = ends(block, axis, shifts)
    excess = jnp.where(where == 0, 0.0, spin(excess, 1, axis))
    behind = jnp.where(where >= blocks - 1, 0.0, spin(behind, -1, axis))
    ups, downs, excesses, behinds = [], [], [], []
    for conduct in conducts:
        up = conduct / (excess + conduct)
        excess = 1.0 + up * excess
        ups.append(up)
        excesses.append(excess)
    for conduct in reversed(conducts):
        down = conduct / (1.0 + behind + conduct)
        behinds.append(behind)
        downs.append(down)
        behind = down * (1.0 + behind)
    downs, behinds = downs[::-1], behinds[::-1]
    inverses = [1.0 / (e + h) for e, h in zip(excesses, behinds)]
    up_all = [ups[0]]
    for up in ups[1:]:
        up_all.append(up_all[-1] * up)
    down_all = [downs[-1]]
    for down in downs[-2::-1]:
        down_all.append(down_all[-1] * down)
    down_all = down_all[::-1]
    into_up = [m * inverse for m, inverse in zip(up_all, inverses)]
    into_down = [m * inverse for m, inverse in zip(down_all[1:] + [1.0], inverses)]
    if axis == LANE:
        into_up = [m * spin(passed_up, 1, axis) for m in into_up]
        into_down = [m * spin(passed_down, -1, axis) for m in into_down]
        used = where < blocks
        steps = [jnp.where(used, 1.0 / m, 0.0) for m in (passed_up, passed_down)]
        return ups, downs, inverses, into_up, into_down, steps
    up_s = jnp.where(where == 0, 0.0, up_all[-1])
    down_s = jnp.where(where >= blocks - 1, 0.0, down_all[0])
    steps = []
    for s in shifts:
        steps.append((up_s, down_s))
        up_s = up_s * spin(up_s, s, axis)
        down_s = down_s * spin(down_s, -s, axis)
    return ups, downs, inverses, into_up, into_down, steps


def earlier_and_later():
    blank = jnp.zeros((2 * LANES, 2 * LANES), f32)
    row, column = place(blank, 0), place(blank, 1)
    ahead = jnp.where(column < LANES, column - row, row - column)
    return jnp.where(ahead > 0, 1.0, 0.0).astype(jnp.bfloat16)


def summed(ups, downs, sums):
    rows = ups.shape[0] * ups.shape[1]
    rest = jnp.concatenate([ups.reshape(rows, LANES), downs.reshape(rows, LANES)], 1)
    pieces = []
    for _ in range(3):
        pieces.append(rest.astype(jnp.bfloat16))
        rest = rest - pieces[-1].astype(f32)
    got = jnp.dot(jnp.concatenate(pieces, 0), sums, preferred_element_type=f32)
    got = got[:rows] + (got[rows : 2 * rows] + got[2 * rows :])
    return got[:, :LANES].reshape(ups.shape), got[:, LANES:].reshape(ups.shape)


def line_solve(values, terms, axis, blocks, shifts, sums=None):
    ups, downs, inverses, into_up, into_down, steps = terms
    where = place(values[0], axis)
    ahead = [values[0]]
    for value, up in zip(values[1:], ups[1:]):
        ahead.append(value + up * ahead[-1])
    back = [downs[-1] * values[-1]]
    for value, down in zip(values[-2::-1], downs[-2::-1]):
        back.append(down * (value + back[-1]))
    back = back[::-1]
    up_in, down_in = ahead[-1], back[0]
    if axis == LANE:
        up_in, down_in = summed(up_in * steps[0], down_in * steps[1], sums)
    else:
        for s, (up_s, down_s) in zip(shifts, steps):
            up_in = up_in + up_s * spin(up_in, s, axis)
            down_in = down_in + down_s * spin(down_in, -s, axis)
        up_in = jnp.where(where == 0, 0.0, spin(up_in, 1, axis))
        down_in = jnp.where(where >= blocks - 1, 0.0, spin(down_in, -1, axis))
    solved = []
    for n, value in enumerate(ahead):
        here = value + back[n + 1] if n + 1 < len(back) else value
        solved.append(here * inverses[n] + into_up[n] * up_in + into_down[n] * down_in)
    return solved


LANE = 2
X_LINE = (1, PEERS_X, (1, 2, 4))
Y_LINE = (LANE, PEERS_Y, (1, 2, 4, 8, 16, 32, 64))


def turned(lists):
    return [jnp.stack([m[n] for m in lists]) for n in range(lists[0].shape[0])]


def slots(field, fill):
    low, high = field[:, :LANES], field[:, LANES:]
    lane = place(low, 1)
    rest = jnp.where(lane < 32, spin(low, 32, 1), spin(high, 64, 1))
    return low, high, jnp.where(lane < 64, rest, fill)


def mix_kernel(*refs):
    given, out, (chi, sigma, vertical, kx, ky), done = refs[:5], refs[5], refs[6:11], refs[11]
    copies = [
        pltpu.make_async_copy(source, target, done.at[n])
        for n, (source, target) in enumerate(zip(given, (chi, sigma, vertical, kx, ky)))
    ]
    for n in (2, 0, 1, 3, 4):
        copies[n].start()
    for copy in copies[:3]:
        copy.wait()
    scaled = (sigma[...] * chi[...]).reshape(CELLS, WIDTH)
    blank = jnp.zeros((64, 64), f32)
    halves = []
    for h in range(2):
        weight = jnp.concatenate(
            [
                jnp.concatenate([vertical[2 * h], blank], 1),
                jnp.concatenate([blank, vertical[2 * h + 1]], 1),
            ],
            0,
        )
        halves.append(
            jnp.dot(
                scaled[:, h * LANES : (h + 1) * LANES],
                weight,
                precision=lax.Precision.HIGHEST,
                preferred_element_type=f32,
            )
        )
    mixed = jnp.concatenate(halves, 1)
    for copy in copies[3:]:
        copy.wait()
    parts = [
        slots(mixed, 0.0),
        slots(kx[...].reshape(CELLS, WIDTH), 1.0),
        slots(ky[...].reshape(CELLS, WIDTH), 1.0),
    ]
    blank = jnp.zeros((CELLS, LANES), f32)
    for c in range(SLOTS):
        block = jnp.concatenate([part[c] for part in parts] + [blank], 0).T
        out[strided(c, PEERS_Y, SLOTS), :] = block[:PEERS_Y]


def deal_kernel(lines, out):
    spare = jnp.zeros((LANES - PEERS_Y, LANES), f32)
    blocks = []
    for c in range(SLOTS):
        block = jnp.concatenate([lines[strided(c, PEERS_Y, SLOTS), :], spare], 0).T[:USED]
        head, tail = block[:SENT], block[SENT:]
        moved = jnp.concatenate([spin(tail, USED - n * CELLS, 1) for n in range(PARTS)], 0)
        blocks.append(jnp.where(place(head, 1) < USED, head, moved))
    for q in range(PEERS_X):
        out[q] = blocks[q % SLOTS]


def dealt(block):
    lane = place(block[:TAIL], 1)
    tail = jnp.zeros((TAIL, LANES), f32)
    for n in reversed(range(PARTS)):
        moved = spin(block[n * TAIL : (n + 1) * TAIL], n * CELLS - USED, 1)
        tail = jnp.where(lane < (n + 1) * CELLS, moved, tail)
    return jnp.concatenate([block, tail], 0)


def solve_kernel(got, out, rows):
    for q in range(PEERS_X):
        block = dealt(got[q])
        for n in range(PARTS * ROWS):
            rows[strided(n * SPAN * PEERS_X + q, SPAN, PEERS_X), :] = block[n * SPAN : (n + 1) * SPAN]

    def field(n):
        at = [[((n * ROWS + j) * SPAN + i) * PEERS_X for j in range(ROWS)] for i in range(SPAN)]
        return [[rows[m : m + PEERS_X, :] for m in some] for some in at]

    sums = earlier_and_later()
    u = [jnp.stack(m) for m in field(0)]
    x_terms = line_terms([jnp.stack(m) for m in field(1)], *X_LINE)
    y_terms = line_terms(turned([jnp.stack(m) for m in field(2)]), *Y_LINE)
    for _ in range(3):
        u = turned(line_solve(u, x_terms, *X_LINE))
        u = turned(line_solve(u, y_terms, *Y_LINE, sums))
    for i in range(SPAN):
        for j in range(ROWS):
            at = (j * SPAN + i) * PEERS_X
            rows[at : at + PEERS_X, :] = u[i][j]
    lane = place(u[0][0], 1)
    for q in range(PEERS_X):
        *head, tail = (rows[strided(j * SPAN * PEERS_X + q, SPAN, PEERS_X), :] for j in range(ROWS))
        for j, value in enumerate(head):
            moved = spin(tail, USED - j * CELLS, 1)
            out[q, j * SPAN : (j + 1) * SPAN, :] = jnp.where(lane < USED, value, moved)


def turn_kernel(got, out):
    blank = jnp.zeros((LANES - SLOTS * CELLS, LANES), f32)
    lane = place(jnp.zeros((SPAN, LANES), f32), 1)
    blocks = []
    for c in range(SLOTS):
        tail = jnp.zeros((SPAN, LANES), f32)
        for j in reversed(range(PARTS)):
            moved = spin(got[c, j * SPAN : (j + 1) * SPAN, :], j * CELLS - USED, 1)
            tail = jnp.where(lane < (j + 1) * CELLS, moved, tail)
        blocks += [got[c], tail]
    out[...] = jnp.concatenate(blocks + [blank], 0).T[:PEERS_Y]


def back_kernel(lines, out):
    blank = jnp.zeros((LANES - PEERS_Y, LANES), f32)
    block = jnp.concatenate([lines[...], blank], 0).T
    low, high, rest = (block[c * CELLS : (c + 1) * CELLS] for c in range(SLOTS))
    lane = place(low, 1)
    low = jnp.where(lane < PEERS_Y, low, spin(rest, 96, 1))
    high = jnp.where(lane < PEERS_Y, high, spin(rest, 64, 1))
    out[...] = jnp.concatenate([low, high], 1).reshape(ROWS, SPAN, WIDTH)


def call(kernel, shape, args, name, scratch=(), space=pltpu.VMEM):
    return pl.pallas_call(
        kernel,
        out_shape=jax.ShapeDtypeStruct(shape, f32),
        in_specs=[pl.BlockSpec(memory_space=space)] * len(args),
        out_specs=pl.BlockSpec(memory_space=pltpu.VMEM),
        scratch_shapes=scratch,
        compiler_params=pltpu.CompilerParams(vmem_limit_bytes=16 << 20),
        name=name,
    )(*args)


def swapped(value, axis):
    return lax.all_to_all(value, axis, split_axis=0, concat_axis=0, tiled=True)


def body(chi, sigma, vertical, kx, ky):
    given = (chi, sigma, vertical, kx, ky)
    given = tuple(pltpu.with_memory_space_constraint(m, pltpu.HBM) for m in given)
    lines = call(
        mix_kernel,
        (PEERS_Y * SLOTS, LANES),
        given,
        "mix",
        [pltpu.VMEM(m.shape, f32) for m in given] + [pltpu.SemaphoreType.DMA((5,))],
        pl.ANY,
    )
    lines = swapped(lines.reshape(PEERS_Y, 1, SLOTS * LANES), "gy").reshape(lines.shape)
    planes = call(deal_kernel, (PEERS_X, SENT, LANES), (lines,), "deal")
    planes = swapped(planes, "gx")
    planes = call(
        solve_kernel,
        (PEERS_X, CELLS - SPAN, LANES),
        (planes,),
        "solve",
        [pltpu.VMEM((PEERS_X * USED, LANES), f32)],
    )
    planes = swapped(planes, "gx")
    lines = call(turn_kernel, (PEERS_Y, LANES), (planes,), "turn")
    lines = swapped(lines, "gy")
    return call(back_kernel, (ROWS, SPAN, WIDTH), (lines,), "back")


def solution(mesh):
    field = P("gy", "gx", None)
    return jax.shard_map(
        body,
        mesh=mesh,
        in_specs=(field, field, P(), field, field),
        out_specs=field,
        check_vma=False,
    )
```
